32 devices in a mesh: space: 8 (over z, y), leaf: 4 (over x, core).
Axes of the slice: x: 2, y: 2, z: 4, core: 2. Of those that a mesh axis runs over, the one named last changes fastest.
Arguments:
- charges: bfloat16 [16, 262144], P(None, ('space', 'leaf')), may hold values from -6 to 6
- leaf_basis: bfloat16 [2048, 64, 128], P(('space', 'leaf')), may hold values from -0.5 to 0.5
- transfer_one: bfloat16 [256, 64, 512], P(('space', 'leaf')), may hold values from -0.25 to 0.25
- transfer_two: bfloat16 [32, 64, 512], P(('space', 'leaf')), may hold values from -0.25 to 0.25
- nodes_leaf: bfloat16 [2048, 3, 64], P(('space', 'leaf')), may hold values from 0 to 6
- nodes_one: bfloat16 [256, 3, 64], P(('space', 'leaf')), may hold values from 0 to 6
- nodes_two: bfloat16 [32, 3, 64], P(('space', 'leaf')), may hold values from 0 to 6
- links_leaf: int32 [2048, 96], P(('space', 'leaf')), may hold values from -1 to 2047, as said below
- links_one: int32 [256, 96], P(('space', 'leaf')), may hold values from -1 to 255, as said below
- links_two: int32 [32, 96], P(('space', 'leaf')), may hold values from -1 to 31, as said below
Outputs:
- potentials: bfloat16 [16, 262144], P(None, ('space', 'leaf'))
The draws below stay inside these ranges and needn't reach their ends.
Inputs may be any that keep to these rules, and one draw needn't show every extreme that they name: `links_leaf`: A live source leaf lies on a device whose space index differs from that of the target leaf's device by at most one; live slots of a row come first. `links_one`: A live source cluster lies on a device whose space index differs from that of the target's device by at most one; live slots of a row come first. `links_two`: live slots of a row come first.
All inputs are finite; a program needn't handle non-finite values.
Results may differ from the reference program's by a relative error of at most 0.007.
Values may be sent and summed in bfloat16 or wider, within the bound.
No kernel may reach another device: no remote copies, remote signals or barrier semaphores. Data moves between devices by JAX's collectives and lax.ppermute only.
A program may use at most 128 MiB of HBM per device.

```python
import jax
import jax.numpy as jnp
from jax import lax

NV = 16
LEAF = 128
K = 64
SLOTS = 96
LEAF_DEV = 64
LEAVES = 2048
POINTS = 262144
CLUSTERS_ONE = 256
CLUSTERS_TWO = 32
N_SPACE = 8
N_LEAF = 4


def make_links(key, targets, per_dev, reach):
    keys = jax.random.split(key, 5)
    target_ids = jnp.arange(targets, dtype=jnp.int32)
    device = target_ids // per_dev
    space_id = device // N_LEAF
    step_space = jax.random.randint(keys[0], (targets, SLOTS), -1, 2)
    if reach == 1:
        src_space = jnp.clip(space_id[:, None] + step_space, 0, N_SPACE - 1)
        src_leaf = jax.random.randint(keys[1], (targets, SLOTS), 0, N_LEAF)
    else:
        src_space = jax.random.randint(keys[0], (targets, SLOTS), 0, N_SPACE)
        src_leaf = jax.random.randint(keys[1], (targets, SLOTS), 0, N_LEAF)
    local = jax.random.randint(keys[2], (targets, SLOTS), 0, per_dev)
    source = (src_space * N_LEAF + src_leaf) * per_dev + local
    device_count = jax.random.randint(keys[3], (N_SPACE * N_LEAF,), SLOTS // 2, SLOTS + 1)
    lower = jax.random.randint(keys[4], (targets,), 0, SLOTS // 8 + 1)
    count = jnp.maximum(device_count[device] - lower, 1)
    count = count.at[0].set(1)
    live = jnp.arange(SLOTS, dtype=jnp.int32)[None, :] < count[:, None]
    source = jnp.where(live, source, -1)
    source = source.at[targets - 2, 0].set(targets - 1)
    return source.astype(jnp.int32)


def draw_links_leaf(key, part):
    return make_links(jax.random.fold_in(key, 11), LEAVES, LEAF_DEV, 1)


def draw_links_one(key, part):
    return make_links(jax.random.fold_in(key, 12), CLUSTERS_ONE, LEAF_DEV // 8, 1)


def draw_links_two(key, part):
    return make_links(jax.random.fold_in(key, 13), CLUSTERS_TWO, LEAF_DEV // 64, 2)


def steps_of(stream_key, shape, cuts, low, largest):
    def one(axis_at, parts):
        steps = jax.random.uniform(jax.random.fold_in(jax.random.fold_in(stream_key, 6), axis_at), (parts,), jnp.float32, low / len(cuts), largest / len(cuts))
        return jnp.repeat(jnp.exp(steps), shape[axis_at] // parts).reshape((-1,) + (1,) * (len(shape) - axis_at - 1))

    factor_of = one(*cuts[0])
    for cut in cuts[1:]:
        factor_of = factor_of * one(*cut)
    return factor_of


def bell_draw(key, shape, deviation, bound, cuts=(), kind=jnp.bfloat16):
    values = jax.random.normal(key, shape, jnp.float32) * deviation
    if len(cuts) > 0:
        values = steps_of(key, shape, cuts, -0.22, 0.18) * values
    return jnp.clip(values, min=-bound, max=bound).astype(kind)


def setup_inputs(seed: int = 0) -> dict:
    seeds = jax.random.split(jax.random.key(seed), 11)
    return {
        "charges": bell_draw(seeds[0], (NV, POINTS), 1.0, 6.0, ((1, 32),)),
        "leaf_basis": bell_draw(seeds[1], (LEAVES, K, LEAF), LEAF ** -0.5, 0.5, ((0, 32),)),
        "transfer_one": bell_draw(seeds[2], (CLUSTERS_ONE, K, 8 * K), (8 * K) ** -0.5, 0.25, ((0, 32),)),
        "transfer_two": bell_draw(seeds[3], (CLUSTERS_TWO, K, 8 * K), (8 * K) ** -0.5, 0.25, ((0, 32),)),
        "nodes_leaf": jnp.clip(6.0 * jax.random.uniform(seeds[4], (LEAVES, 3, K), jnp.float32) ** steps_of(seeds[4], (LEAVES, 3, K), ((0, 32),), -0.2, 0.2), 0.0, 6.0).astype(jnp.bfloat16),
        "nodes_one": jnp.clip(6.0 * jax.random.uniform(seeds[5], (CLUSTERS_ONE, 3, K), jnp.float32) ** steps_of(seeds[5], (CLUSTERS_ONE, 3, K), ((0, 32),), -0.2, 0.2), 0.0, 6.0).astype(jnp.bfloat16),
        "nodes_two": jnp.clip(6.0 * jax.random.uniform(seeds[6], (CLUSTERS_TWO, 3, K), jnp.float32) ** steps_of(seeds[6], (CLUSTERS_TWO, 3, K), ((0, 32),), -0.2, 0.2), 0.0, 6.0).astype(jnp.bfloat16),
        "links_leaf": draw_links_leaf(jax.random.fold_in(seeds[10], 71), 0),
        "links_one": draw_links_one(jax.random.fold_in(seeds[10], 71), 0),
        "links_two": draw_links_two(jax.random.fold_in(seeds[10], 71), 0),
    }


SQRT_THREE = 1.7320508075688772
LENGTH = 2.0
AMPLITUDE = 0.25

def matern_block(target_nodes, source_nodes):
    diff = target_nodes[:, None, :, :, None] - source_nodes[:, :, :, None, :]
    dist = jnp.sqrt(lax.optimization_barrier(jnp.sum(diff * diff, axis=2))) * (SQRT_THREE / LENGTH)
    return (AMPLITUDE * (1.0 + dist) * jnp.exp(-dist)).astype(jnp.bfloat16)

def couple(coeffs, nodes, links, target_nodes, group):
    count = links.shape[0]
    slots = links.shape[1]
    rank = coeffs.shape[1]
    width = coeffs.shape[2]
    live = links >= 0
    safe = jnp.where(live, links, 0).astype(jnp.int32)

    def one_group(args):
        index, alive, tnodes = args
        picked = jnp.where(alive[:, :, None, None], coeffs[index], jnp.zeros((), jnp.bfloat16))
        source_nodes = nodes[index].astype(jnp.float32)
        matrix = matern_block(tnodes.astype(jnp.float32), source_nodes)
        return jnp.einsum('gjab,gjbv->gav', matrix.astype(jnp.float32), picked.astype(jnp.float32))
    result = lax.map(one_group, (safe.reshape(-1, group, slots), live.reshape(-1, group, slots), target_nodes.reshape(-1, group, 3, rank)))
    return result.reshape(count, rank, width)

def reference(charges, leaf_basis, transfer_one, transfer_two, nodes_leaf, nodes_one, nodes_two, links_leaf, links_one, links_two):
    leaves = leaf_basis.shape[0]
    rank = leaf_basis.shape[1]
    leaf_size = leaf_basis.shape[2]
    width = charges.shape[0]
    shaped = charges.reshape(width, leaves, leaf_size)
    coef_leaf = jnp.einsum('tkp,vtp->tkv', leaf_basis.astype(jnp.float32), shaped.astype(jnp.float32)).astype(jnp.bfloat16)
    count_one = leaves // 8
    count_two = leaves // 64
    coef_one = jnp.einsum('pkm,pmv->pkv', transfer_one.astype(jnp.float32), coef_leaf.reshape(count_one, 8 * rank, width).astype(jnp.float32)).astype(jnp.bfloat16)
    coef_two = jnp.einsum('pkm,pmv->pkv', transfer_two.astype(jnp.float32), coef_one.reshape(count_two, 8 * rank, width).astype(jnp.float32)).astype(jnp.bfloat16)
    far_leaf = couple(coef_leaf, nodes_leaf, links_leaf, nodes_leaf, 16)
    far_one = couple(coef_one, nodes_one, links_one, nodes_one, 8)
    far_two = couple(coef_two, nodes_two, links_two, nodes_two, 1)
    local_two = far_two.astype(jnp.bfloat16)
    down_one = jnp.einsum('pkm,pkv->pmv', transfer_two.astype(jnp.float32), local_two.astype(jnp.float32))
    local_one = (far_one + down_one.reshape(count_one, rank, width)).astype(jnp.bfloat16)
    down_leaf = jnp.einsum('pkm,pkv->pmv', transfer_one.astype(jnp.float32), local_one.astype(jnp.float32))
    local_leaf = (far_leaf + down_leaf.reshape(leaves, rank, width)).astype(jnp.bfloat16)
    result = jnp.einsum('tkp,tkv->vtp', leaf_basis.astype(jnp.float32), local_leaf.astype(jnp.float32))
    return result.reshape(width, leaves * leaf_size).astype(jnp.bfloat16)
```

```python
import functools

import jax
import jax.numpy as jnp
from jax import lax
from jax.experimental import pallas as pl
from jax.experimental.pallas import tpu as pltpu
from jax.sharding import PartitionSpec as P

LOG2E = 1.4426950408889634
SCALE = 0.75
AMPLITUDE = 0.25
CHUNK = 16
UNROLL = 4
F32 = jnp.float32
BF16 = jnp.bfloat16
NT = (((1,), (1,)), ((), ()))


def dot_nt(a, b):
    return lax.dot_general(a, b, NT, preferred_element_type=F32)


def low_half(shape):
    return lax.broadcasted_iota(jnp.int32, shape, 1) < shape[1] // 2


def wide_nodes(ref, pair, count):
    if count == 1:
        one = ref[0].astype(F32)
        return jnp.concatenate([one, one], axis=1)
    return jnp.concatenate([ref[2 * pair].astype(F32), ref[2 * pair + 1].astype(F32)], axis=1)


def split(value):
    high = value.astype(BF16).astype(F32)
    rest = value - high
    middle = rest.astype(BF16).astype(F32)
    return high, middle, rest - middle


def norm_of(nodes):
    square = nodes * nodes
    return (square[0:1] + square[1:2] + square[2:3]) * SCALE


def up_kernel(counts, charges, basis, t_one, t_two, n_leaf, n_one, n_two, pack):
    leaf_dev, one_dev, two_dev = counts
    lanes = 0
    for nodes_ref, count in ((n_leaf, leaf_dev), (n_one, one_dev), (n_two, two_dev)):
        for pair in range((count + 1) // 2):
            nodes = wide_nodes(nodes_ref, pair, count)
            ones = jnp.ones((2, 128), F32)
            rows = jnp.concatenate([nodes, *split(norm_of(nodes)), ones], axis=0)
            pack[0:8, lanes : lanes + 128] = rows.astype(BF16)
            lanes += 128
    half = low_half((16, 128))
    for pair in range(leaf_dev // 2):
        at = pair * 256
        both = jnp.concatenate([charges[:, at : at + 128], charges[:, at + 128 : at + 256]], axis=0)
        coef = dot_nt(both, basis[pair * 128 : pair * 128 + 128, :])
        coef = jnp.where(half, coef[:16], coef[16:])
        pack[8:24, pair * 128 : pair * 128 + 128] = coef.astype(BF16)
    start = leaf_dev * 64
    for pair in range(one_dev // 2):
        at = pair * 1024
        both = jnp.concatenate([pack[8:24, at : at + 512], pack[8:24, at + 512 : at + 1024]], axis=0)
        coef = dot_nt(both, t_one[pair * 128 : pair * 128 + 128, :])
        coef = jnp.where(half, coef[:16], coef[16:])
        pack[8:24, start + pair * 128 : start + pair * 128 + 128] = coef.astype(BF16)
    below, start = start, start + one_dev * 64
    for pair in range((two_dev + 1) // 2):
        parts = []
        for q in range(2 * pair, 2 * pair + 2):
            q = min(q, two_dev - 1)
            children = pack[8:24, below + q * 512 : below + q * 512 + 512]
            parts.append(dot_nt(children, t_two[q * 64 : q * 64 + 64, :]))
        coef = jnp.concatenate(parts, axis=1)
        pack[8:24, start + pair * 128 : start + pair * 128 + 128] = coef.astype(BF16)


def target_kernel(counts, n_leaf, n_one, n_two, out):
    row = 0
    for nodes_ref, count in zip((n_leaf, n_one, n_two), counts):
        for pair in range((count + 1) // 2):
            nodes = wide_nodes(nodes_ref, pair, count)
            cross = nodes * (-2.0 * SCALE)
            high = cross.astype(BF16).astype(F32)
            n1, n2, n3 = split(norm_of(nodes))
            one = jnp.ones((3, 128), F32)
            zero = jnp.zeros((3, 128), F32)
            rows = jnp.concatenate([high, one, n1, n2, cross - high, zero, n3, zero[0:1]], axis=0)
            out[row : row + 128, :] = rows.T.astype(BF16)
            row += 128


def matern(square):
    value = jnp.maximum(square, 1e-30)
    r = value * lax.rsqrt(value)
    return (r + 1.0) * jnp.exp2(r * (-LOG2E))


def gather_features(table, links, base, half):
    tiles = []
    for g in range(CHUNK // 2):
        first, second = links[base + 2 * g], links[base + 2 * g + 1]
        tile = jnp.where(half, table[first, 0:8, :], table[second, 0:8, :])
        tiles.append(jnp.concatenate([tile, tile], axis=0))
    return jnp.concatenate(tiles, axis=1)


def gather_coefs(table, links, base, half):
    tiles = []
    for g in range(CHUNK // 2):
        first, second = links[base + 2 * g], links[base + 2 * g + 1]
        tiles.append(jnp.where(half, table[first, 8:24, :], table[second, 8:24, :]))
    return jnp.concatenate(tiles, axis=1)


def widen(tile):
    swapped = jnp.concatenate([tile[:, 64:], tile[:, :64]], axis=1)
    half = low_half(tile.shape)
    return jnp.where(half, tile, swapped), jnp.where(half, swapped, tile)


def couple_kernel(counts, sizes, targets, slots, links, chunks, bases, features, *refs):
    leaf_dev, one_dev, _ = counts
    blocks, far = refs[: len(sizes)], refs[len(sizes)]
    table = refs[len(sizes) + 1]
    dbufs = refs[len(sizes) + 2 : len(sizes) + 2 + UNROLL]
    kbufs = refs[len(sizes) + 2 + UNROLL :]
    far[...] = jnp.zeros_like(far)
    table[table.shape[0] - 1] = jnp.zeros((24, 128), BF16)
    at = 0
    for ref, size in zip(blocks, sizes):
        for index in range(size):
            for first, count, slot in ((0, leaf_dev, 2 * at), (leaf_dev, one_dev, 2 * at + 1)):
                base = bases[slot]

                def one_pair(pair, carry, ref=ref, index=index, first=first, base=base):
                    lane = pl.multiple_of((first // 2 + pair) * 128, 128)
                    low, high = widen(ref[index, :, pl.ds(lane, 128)])
                    table[base + 2 * pair] = low
                    table[base + 2 * pair + 1] = high
                    return carry

                lax.fori_loop(0, count // 2, one_pair, 0, unroll=4)
            at += 1
    half8 = low_half((8, 128))
    half16 = low_half((16, 128))
    last_target = targets - 1

    def step(u, state):
        t0, c0, t1, b1, t2, b2 = state
        d_in, d_out = dbufs[u - 1], dbufs[u]
        k_in, k_out = kbufs[u - 1], kbufs[u]
        tt = jnp.minimum(t0, last_target)
        b0 = tt * slots + c0 * CHUNK
        row = pl.multiple_of(tt * 64, 64)
        d_out[...] = jnp.dot(
            features[pl.ds(row, 64), :],
            gather_features(table, links, b0, half8),
            preferred_element_type=F32,
        )
        coefs = gather_coefs(table, links, b2, half16)
        far[t2] = far[t2] + dot_nt(coefs, k_in[...].astype(BF16))
        for g in range(CHUNK // 2):
            k_out[:, g * 128 : g * 128 + 128] = matern(d_in[:, g * 128 : g * 128 + 128])
        last = c0 + 1 >= chunks[tt]
        next_t = jnp.where(last, jnp.minimum(t0 + 1, targets), t0)
        next_c = jnp.where(last, 0, c0 + 1)
        return next_t, next_c, t0, b0, t1, b1

    def body(_, state):
        for u in range(UNROLL):
            state = step(u, state)
        return state

    zero, none = jnp.int32(0), jnp.int32(targets)
    total = chunks[targets]
    lax.fori_loop(0, (total + 2 + UNROLL - 1) // UNROLL, body, (zero, zero, none, zero, none, zero))


def down_kernel(counts, n_blocks, slots, links, bases, features, blocks, far, basis, t_one, t_two, out, table):
    leaf_dev, one_dev, two_dev = counts
    pairs = (two_dev + 1) // 2
    table[table.shape[0] - 1] = jnp.zeros((24, 128), BF16)
    for index in range(n_blocks):
        base = bases[index]
        for pair in range(pairs):
            low, high = widen(blocks[index, :, pair * 128 : pair * 128 + 128])
            table[base + 2 * pair] = low
            if two_dev > 1:
                table[base + 2 * pair + 1] = high
    half8 = low_half((8, 128))
    half16 = low_half((16, 128))
    for q in range(two_dev):
        far_two = jnp.zeros((16, 64), F32)
        for c in range(slots // CHUNK):
            base = q * slots + c * CHUNK
            square = jnp.dot(
                features[q * 64 : q * 64 + 64, :],
                gather_features(table, links, base, half8),
                preferred_element_type=F32,
            )
            far_two += dot_nt(gather_coefs(table, links, base, half16), matern(square).astype(BF16))
        local_two = (far_two * AMPLITUDE).astype(BF16)
        down_one = jnp.dot(local_two, t_two[q * 64 : q * 64 + 64, :], preferred_element_type=F32)
        for i in range(8):
            p = q * 8 + i
            local_one = far[leaf_dev + p] * AMPLITUDE + down_one[:, i * 64 : i * 64 + 64]
            down_leaf = jnp.dot(
                local_one.astype(BF16), t_one[p * 64 : p * 64 + 64, :], preferred_element_type=F32
            )
            for j in range(8):
                t = p * 8 + j
                local_leaf = far[t] * AMPLITUDE + down_leaf[:, j * 64 : j * 64 + 64]
                out[:, t * 128 : t * 128 + 128] = jnp.dot(
                    local_leaf.astype(BF16), basis[t * 64 : t * 64 + 64, :], preferred_element_type=F32
                ).astype(BF16)


VMEM = pl.BlockSpec(memory_space=pltpu.VMEM)
SMEM = pl.BlockSpec(memory_space=pltpu.SMEM)


def call(kernel, name, specs, out, scratch, flops, args):
    moved = sum(a.size * a.dtype.itemsize for a in args)
    return pl.pallas_call(
        kernel,
        name=name,
        out_shape=out,
        in_specs=specs,
        out_specs=VMEM,
        scratch_shapes=scratch,
        cost_estimate=pl.CostEstimate(flops=flops, bytes_accessed=moved, transcendentals=0),
        compiler_params=pltpu.CompilerParams(vmem_limit_bytes=60 * 2**20),
    )(*args)


def swap(value, axis, mask):
    count = lax.axis_size(axis)
    return lax.ppermute(value, axis, [(i, i ^ mask) for i in range(count)])


def swap_outer(value):
    count = lax.axis_size("space")
    pairs = []
    for s in range(count):
        other = s + 1 if s % 2 else s - 1
        pairs.append((s, other if 0 <= other < count else s))
    return lax.ppermute(value, "space", pairs)


def spread(group, masks, axis):
    order = [0]
    for mask in masks:
        merged = group[0] if len(group) == 1 else jnp.concatenate(group, axis=0)
        group = group + [swap(merged, axis, mask)]
        order = order + [m ^ mask for m in order]
    return group, order


def powers(count):
    return [1 << b for b in reversed(range(count.bit_length() - 1))]


def local(
    charges,
    leaf_basis,
    transfer_one,
    transfer_two,
    nodes_leaf,
    nodes_one,
    nodes_two,
    links_leaf,
    links_one,
    links_two,
):
    width = charges.shape[0]
    leaf_dev, rank, leaf_size = leaf_basis.shape
    one_dev = leaf_dev // 8
    two_dev = one_dev // 8
    counts = (leaf_dev, one_dev, two_dev)
    slots = links_leaf.shape[1]
    n_space, n_leaf = lax.axis_size("space"), lax.axis_size("leaf")
    my_space, my_leaf = lax.axis_index("space"), lax.axis_index("leaf")
    two_lanes = (two_dev + 1) // 2 * 128
    split_at = (leaf_dev + one_dev) * rank
    lanes = split_at + two_lanes

    basis = leaf_basis.reshape(leaf_dev * rank, leaf_size)
    t_one = transfer_one.reshape(one_dev * rank, 8 * rank)
    t_two = transfer_two.reshape(two_dev * rank, 8 * rank)
    pack = call(
        functools.partial(up_kernel, counts),
        "up",
        [VMEM] * 7,
        jax.ShapeDtypeStruct((24, lanes), BF16),
        [],
        2 * leaf_dev * rank * leaf_size * width,
        (charges, basis, t_one, t_two, nodes_leaf, nodes_one, nodes_two),
    )
    feature_rows = (leaf_dev + one_dev) * rank + two_lanes
    features = call(
        functools.partial(target_kernel, counts),
        "targets",
        [VMEM] * 3,
        jax.ShapeDtypeStruct((feature_rows, 16), BF16),
        [],
        2**20,
        (nodes_leaf, nodes_one, nodes_two),
    )

    own = pack[None]
    outer = jnp.concatenate([swap(own, "space", 1), swap_outer(own)], axis=0)
    own_group, order = spread([own], powers(n_leaf), "leaf")
    outer_group, _ = spread([outer], powers(n_leaf), "leaf")
    sizes = tuple(a.shape[0] for a in own_group + outer_group)

    even = my_space % 2 == 0
    inner_side = jnp.where(even, 2, 0)
    outer_side = jnp.where(even, 0, 2)
    sides = [1] * n_leaf + [inner_side, outer_side] * n_leaf
    masks = order + [m for m in order for _ in range(2)]
    n_leaf_rows = 3 * n_leaf * leaf_dev
    n_one_rows = 3 * n_leaf * one_dev
    devices = [side * n_leaf + (my_leaf ^ mask) for side, mask in zip(sides, masks)]
    starts = jnp.stack(devices).astype(jnp.int32)
    bases = jnp.stack([starts * leaf_dev, n_leaf_rows + starts * one_dev], axis=1).reshape(-1)
    empty = n_leaf_rows + n_one_rows
    first_device = (my_space - 1) * n_leaf
    rows = jnp.concatenate(
        [
            jnp.where(links_leaf >= 0, links_leaf - first_device * leaf_dev, empty),
            jnp.where(links_one >= 0, links_one - first_device * one_dev + n_leaf_rows, empty),
        ],
        axis=0,
    ).astype(jnp.int32)
    live = jnp.sum((rows != empty).astype(jnp.int32), axis=1)
    chunks = jnp.maximum((live + CHUNK - 1) // CHUNK, 1)
    chunks = jnp.concatenate([chunks, jnp.sum(chunks)[None]]).astype(jnp.int32)

    targets = leaf_dev + one_dev
    far = call(
        functools.partial(couple_kernel, counts, sizes, targets, slots),
        "couple",
        [SMEM, SMEM, SMEM, VMEM] + [VMEM] * len(sizes),
        jax.ShapeDtypeStruct((targets + 1, width, rank), F32),
        [pltpu.VMEM((empty + 1, 24, 128), BF16)] + [pltpu.VMEM((rank, CHUNK * rank), F32)] * (2 * UNROLL),
        2**34,
        (rows.reshape(-1), chunks, bases, features[: targets * rank], *own_group, *outer_group),
    )

    two = jnp.concatenate([a[:, :, split_at:] for a in own_group], axis=0)
    two_group, two_order = [two], [0]
    for mask in powers(n_space):
        two_group = [jnp.concatenate(two_group + [swap(two_group[0], "space", mask)], axis=0)]
        two_order = two_order + [m ^ mask for m in two_order]
    two_bases = jnp.stack(
        [((my_space ^ sm) * n_leaf + (my_leaf ^ lm)) * two_dev for sm in two_order for lm in order]
    ).astype(jnp.int32)
    n_two = n_space * n_leaf * two_dev
    rows_two = jnp.where(links_two >= 0, links_two, n_two).astype(jnp.int32).reshape(-1)
    return call(
        functools.partial(down_kernel, counts, n_space * n_leaf, slots),
        "down",
        [SMEM, SMEM] + [VMEM] * 6,
        jax.ShapeDtypeStruct((width, leaf_dev * leaf_size), BF16),
        [pltpu.VMEM((n_two + 1, 24, 128), BF16)],
        2**24,
        (rows_two, two_bases, features[targets * rank :], two_group[0], far, basis, t_one, t_two),
    )


def solution(mesh):
    return jax.shard_map(
        local,
        mesh=mesh,
        in_specs=(
            P(None, ("space", "leaf")),
            P(("space", "leaf"), None, None),
            P(("space", "leaf"), None, None),
            P(("space", "leaf"), None, None),
            P(("space", "leaf"), None, None),
            P(("space", "leaf"), None, None),
            P(("space", "leaf"), None, None),
            P(("space", "leaf"), None),
            P(("space", "leaf"), None),
            P(("space", "leaf"), None),
        ),
        out_specs=P(None, ("space", "leaf")),
        check_vma=False,
    )
```

```python
import functools

import jax
import jax.numpy as jnp
from jax import lax
from jax.experimental import pallas as pl
from jax.experimental.pallas import tpu as pltpu
from jax.sharding import PartitionSpec as P


LOG2E = 1.4426950408889634
SCALE = 0.75
AMPLITUDE = 0.25
CHUNK = 16
UNROLL = 6
F32 = jnp.float32
BF16 = jnp.bfloat16
NT = (((1,), (1,)), ((), ()))


def dot_nt(a, b):
    return lax.dot_general(a, b, NT, preferred_element_type=F32)


def low_half(shape):
    return lax.broadcasted_iota(jnp.int32, shape, 1) < shape[1] // 2


def wide_nodes(ref, pair, count):
    if ref.shape[0] == count:
        parts = [ref[min(2 * pair + side, count - 1)] for side in range(2)]
    else:
        parts = [ref[:, 2 * pair + side, :] for side in range(2)]
    return jnp.concatenate([part.astype(F32) for part in parts], axis=1)


def split(value):
    high = value.astype(BF16).astype(F32)
    rest = value - high
    middle = rest.astype(BF16).astype(F32)
    return high, middle, rest - middle


def norm_of(nodes):
    square = nodes * nodes
    return (square[0:1] + square[1:2] + square[2:3]) * SCALE


def up_kernel(counts, charges, basis, t_one, t_two, n_leaf, n_one, n_two, pack):
    leaf_dev, one_dev, two_dev = counts
    lanes = 0
    for nodes_ref, count in ((n_leaf, leaf_dev), (n_one, one_dev), (n_two, two_dev)):
        for pair in range((count + 1) // 2):
            nodes = wide_nodes(nodes_ref, pair, count)
            ones = jnp.ones((2, 128), F32)
            rows = jnp.concatenate([nodes, *split(norm_of(nodes)), ones], axis=0)
            pack[0:8, lanes : lanes + 128] = rows.astype(BF16)
            lanes += 128
    half = low_half((16, 128))
    for pair in range(leaf_dev // 2):
        at = pair * 256
        both = jnp.concatenate([charges[:, at : at + 128], charges[:, at + 128 : at + 256]], axis=0)
        coef = dot_nt(both, basis[pair * 128 : pair * 128 + 128, :])
        coef = jnp.where(half, coef[:16], coef[16:])
        pack[8:24, pair * 128 : pair * 128 + 128] = coef.astype(BF16)
    start = leaf_dev * 64
    for pair in range(one_dev // 2):
        at = pair * 1024
        both = jnp.concatenate([pack[8:24, at : at + 512], pack[8:24, at + 512 : at + 1024]], axis=0)
        coef = dot_nt(both, t_one[pair * 128 : pair * 128 + 128, :])
        coef = jnp.where(half, coef[:16], coef[16:])
        pack[8:24, start + pair * 128 : start + pair * 128 + 128] = coef.astype(BF16)
    below, start = start, start + one_dev * 64
    for pair in range((two_dev + 1) // 2):
        parts = []
        for q in range(2 * pair, 2 * pair + 2):
            q = min(q, two_dev - 1)
            children = pack[8:24, below + q * 512 : below + q * 512 + 512]
            parts.append(dot_nt(children, t_two[q * 64 : q * 64 + 64, :]))
        coef = jnp.concatenate(parts, axis=1)
        pack[8:24, start + pair * 128 : start + pair * 128 + 128] = coef.astype(BF16)


def prepare_kernel(counts, n_leaf, n_one, n_two, l_leaf, l_one, l_two, gate, main, top, rows, rows_two):
    del gate
    leaf_dev, one_dev, two_dev = counts
    row = 0
    for nodes_ref, count, out in ((n_leaf, leaf_dev, main), (n_one, one_dev, main), (n_two, two_dev, top)):
        if out is top:
            row = 0
        for pair in range((count + 1) // 2):
            nodes = wide_nodes(nodes_ref, pair, count)
            cross = nodes * (-2.0 * SCALE)
            high = cross.astype(BF16).astype(F32)
            n1, n2, n3 = split(norm_of(nodes))
            one = jnp.ones((3, 128), F32)
            zero = jnp.zeros((3, 128), F32)
            tile = jnp.concatenate([high, one, n1, n2, cross - high, zero, n3, zero[0:1]], axis=0)
            out[row : row + 128, :] = tile.T.astype(BF16)
            row += 128
    slots = l_leaf.shape[1]
    axis_leaf = lax.axis_size("leaf")
    first = (lax.axis_index("space") - 1) * axis_leaf
    leaf_rows, one_rows = 3 * axis_leaf * leaf_dev, 3 * axis_leaf * one_dev
    empty = leaf_rows + one_rows
    total = jnp.zeros((1, 1), jnp.int32)
    start = 0
    for ref, shift in ((l_leaf, -first * leaf_dev), (l_one, leaf_rows - first * one_dev)):
        links = ref[...]
        live = links >= 0
        count = jnp.sum(jnp.where(live, 1.0, 0.0), axis=1, keepdims=True).astype(jnp.int32)
        chunks = jnp.maximum((count + (CHUNK - 1)) // CHUNK, 1)
        total = total + jnp.sum(chunks.astype(F32), axis=0, keepdims=True).astype(jnp.int32)
        end = start + links.shape[0]
        rows[start:end, 0:slots] = jnp.where(live, links + shift, empty)
        rows[start:end, slots:] = jnp.broadcast_to(chunks, (links.shape[0], 128 - slots))
        start = end
    rows[start : start + 8, :] = jnp.broadcast_to(total, (8, 128))
    n_top = lax.axis_size("space") * axis_leaf * two_dev
    links = l_two[...]
    rows_two[:, 0:slots] = jnp.where(links >= 0, links, n_top)
    rows_two[:, slots:] = jnp.zeros((two_dev, 128 - slots), jnp.int32)


def matern(square):
    value = jnp.maximum(square, 1e-30)
    r = value * lax.rsqrt(value)
    return (r + 1.0) * jnp.exp2(r * (-LOG2E))


def gather_features(table, links, base, half):
    tiles = []
    for g in range(CHUNK // 2):
        first, second = links[base + 2 * g], links[base + 2 * g + 1]
        tile = jnp.where(half, table[first, 0:8, :], table[second, 0:8, :])
        tiles.append(jnp.concatenate([tile, tile], axis=0))
    return jnp.concatenate(tiles, axis=1)


def gather_coefs(table, links, base, half):
    tiles = []
    for g in range(CHUNK // 2):
        first, second = links[base + 2 * g], links[base + 2 * g + 1]
        tiles.append(jnp.where(half, table[first, 8:24, :], table[second, 8:24, :]))
    return jnp.concatenate(tiles, axis=1)


def widen(tile):
    swapped = jnp.concatenate([tile[:, 64:], tile[:, :64]], axis=1)
    half = low_half(tile.shape)
    return jnp.where(half, tile, swapped), jnp.where(half, swapped, tile)


def couple_kernel(counts, sizes, places, targets, slots, links, features, *refs):
    leaf_dev, one_dev, _ = counts
    axis_leaf = lax.axis_size("leaf")
    my_leaf = lax.axis_index("leaf")
    parity = lax.axis_index("space") % 2
    side_of = (jnp.int32(1), 2 - 2 * parity, 2 * parity)
    starts = (0, 3 * axis_leaf * leaf_dev)
    blocks, far = refs[: len(sizes)], refs[len(sizes)]
    table = refs[len(sizes) + 1]
    dbufs = refs[len(sizes) + 2 : len(sizes) + 2 + UNROLL]
    kbufs = refs[len(sizes) + 2 + UNROLL :]
    far[...] = jnp.zeros_like(far)
    table[table.shape[0] - 1] = jnp.zeros((24, 128), BF16)
    at = 0
    for ref, size in zip(blocks, sizes):
        for index in range(size):
            kind, mask = places[at]
            device = side_of[kind] * axis_leaf + (my_leaf ^ mask)
            for first, count, start in ((0, leaf_dev, starts[0]), (leaf_dev, one_dev, starts[1])):
                base = start + device * count

                def one_pair(pair, carry, ref=ref, index=index, first=first, base=base):
                    lane = pl.multiple_of((first // 2 + pair) * 128, 128)
                    low, high = widen(ref[index, :, pl.ds(lane, 128)])
                    table[base + 2 * pair] = low
                    table[base + 2 * pair + 1] = high
                    return carry

                lax.fori_loop(0, count // 2, one_pair, 0, unroll=4)
            at += 1
    half8 = low_half((8, 128))
    half16 = low_half((16, 128))
    last_target = targets - 1

    def step(u, state):
        t0, c0, t1, b1, t2, b2 = state
        d_in, d_out = dbufs[u - 1], dbufs[u]
        k_in, k_out = kbufs[u - 1], kbufs[u]
        tt = jnp.minimum(t0, last_target)
        b0 = tt * 128 + c0 * CHUNK
        row = pl.multiple_of(tt * 64, 64)
        d_out[...] = jnp.dot(
            features[pl.ds(row, 64), :],
            gather_features(table, links, b0, half8),
            preferred_element_type=F32,
        )
        coefs = gather_coefs(table, links, b2, half16)
        far[t2] = far[t2] + dot_nt(coefs, k_in[...].astype(BF16))
        for g in range(CHUNK // 2):
            k_out[:, g * 128 : g * 128 + 128] = matern(d_in[:, g * 128 : g * 128 + 128])
        last = c0 + 1 >= links[tt * 128 + slots]
        next_t = jnp.where(last, jnp.minimum(t0 + 1, targets), t0)
        next_c = jnp.where(last, 0, c0 + 1)
        return next_t, next_c, t0, b0, t1, b1

    def body(_, state):
        for u in range(UNROLL):
            state = step(u, state)
        return state

    zero, none = jnp.int32(0), jnp.int32(targets)
    total = links[targets * 128]
    lax.fori_loop(0, (total + 2 + UNROLL - 1) // UNROLL, body, (zero, zero, none, zero, none, zero))


def down_kernel(counts, places, slots, links, features, blocks, far, basis, t_one, t_two, out, table):
    leaf_dev, _, two_dev = counts
    pairs = (two_dev + 1) // 2
    table[table.shape[0] - 1] = jnp.zeros((24, 128), BF16)
    axis_leaf = lax.axis_size("leaf")
    my_space, my_leaf = lax.axis_index("space"), lax.axis_index("leaf")
    for index, (space_mask, leaf_mask) in enumerate(places):
        base = ((my_space ^ space_mask) * axis_leaf + (my_leaf ^ leaf_mask)) * two_dev
        for pair in range(pairs):
            low, high = widen(blocks[index, :, pair * 128 : pair * 128 + 128])
            table[base + 2 * pair] = low
            if two_dev > 1:
                table[base + 2 * pair + 1] = high
    half8 = low_half((8, 128))
    half16 = low_half((16, 128))
    for q in range(two_dev):
        far_two = jnp.zeros((16, 64), F32)
        for c in range(slots // CHUNK):
            base = q * 128 + c * CHUNK
            square = jnp.dot(
                features[q * 64 : q * 64 + 64, :],
                gather_features(table, links, base, half8),
                preferred_element_type=F32,
            )
            far_two += dot_nt(gather_coefs(table, links, base, half16), matern(square).astype(BF16))
        local_two = (far_two * AMPLITUDE).astype(BF16)
        down_one = jnp.dot(local_two, t_two[q * 64 : q * 64 + 64, :], preferred_element_type=F32)
        for i in range(8):
            p = q * 8 + i
            local_one = far[leaf_dev + p] * AMPLITUDE + down_one[:, i * 64 : i * 64 + 64]
            down_leaf = jnp.dot(
                local_one.astype(BF16), t_one[p * 64 : p * 64 + 64, :], preferred_element_type=F32
            )
            for j in range(8):
                t = p * 8 + j
                local_leaf = far[t] * AMPLITUDE + down_leaf[:, j * 64 : j * 64 + 64]
                out[:, t * 128 : t * 128 + 128] = jnp.dot(
                    local_leaf.astype(BF16), basis[t * 64 : t * 64 + 64, :], preferred_element_type=F32
                ).astype(BF16)


VMEM = pl.BlockSpec(memory_space=pltpu.VMEM)
SMEM = pl.BlockSpec(memory_space=pltpu.SMEM)


def call(kernel, specs, out, scratch, flops, args):
    moved = sum(a.size * a.dtype.itemsize for a in args)
    return pl.pallas_call(
        kernel,
        out_shape=out,
        in_specs=specs,
        out_specs=jax.tree.map(lambda _: VMEM, out),
        scratch_shapes=scratch,
        cost_estimate=pl.CostEstimate(flops=flops, bytes_accessed=moved, transcendentals=0),
        compiler_params=pltpu.CompilerParams(vmem_limit_bytes=60 * 2**20),
    )(*args)


def swap(value, axis, mask):
    count = lax.axis_size(axis)
    return lax.ppermute(value, axis, [(i, i ^ mask) for i in range(count)])


def swap_outer(value):
    count = lax.axis_size("space")
    pairs = []
    for s in range(count):
        other = s + 1 if s % 2 else s - 1
        pairs.append((s, other if 0 <= other < count else s))
    return lax.ppermute(value, "space", pairs)


def spread(group, masks, axis):
    order = [0]
    for mask in masks:
        merged = group[0] if len(group) == 1 else jnp.concatenate(group, axis=0)
        group = group + [swap(merged, axis, mask)]
        order = order + [m ^ mask for m in order]
    return group, order


def powers(count):
    return [1 << b for b in reversed(range(count.bit_length() - 1))]


def local_body(
    charges,
    leaf_basis,
    transfer_one,
    transfer_two,
    nodes_leaf,
    nodes_one,
    nodes_two,
    links_leaf,
    links_one,
    links_two,
):
    width = charges.shape[0]
    leaf_dev, rank, leaf_size = leaf_basis.shape
    one_dev = leaf_dev // 8
    two_dev = one_dev // 8
    counts = (leaf_dev, one_dev, two_dev)
    slots = links_leaf.shape[1]
    n_space, n_leaf = lax.axis_size("space"), lax.axis_size("leaf")
    two_lanes = (two_dev + 1) // 2 * 128
    split_at = (leaf_dev + one_dev) * rank
    lanes = split_at + two_lanes

    basis = leaf_basis.reshape(leaf_dev * rank, leaf_size)
    t_one = transfer_one.reshape(one_dev * rank, 8 * rank)
    t_two = transfer_two.reshape(two_dev * rank, 8 * rank)
    nodes_leaf, nodes_one = jnp.swapaxes(nodes_leaf, 0, 1), jnp.swapaxes(nodes_one, 0, 1)
    pack = call(
        functools.partial(up_kernel, counts),
        [VMEM] * 7,
        jax.ShapeDtypeStruct((24, lanes), BF16),
        [],
        2 * leaf_dev * rank * leaf_size * width,
        (charges, basis, t_one, t_two, nodes_leaf, nodes_one, nodes_two),
    )
    targets = leaf_dev + one_dev
    main, top, rows, rows_two = call(
        functools.partial(prepare_kernel, counts),
        [VMEM] * 6 + [pl.BlockSpec(memory_space=pl.ANY)],
        (
            jax.ShapeDtypeStruct((targets * rank, 16), BF16),
            jax.ShapeDtypeStruct((two_lanes, 16), BF16),
            jax.ShapeDtypeStruct((targets + 8, 128), jnp.int32),
            jax.ShapeDtypeStruct((two_dev, 128), jnp.int32),
        ),
        [],
        2**32,
        (nodes_leaf, nodes_one, nodes_two, links_leaf, links_one, links_two, pack),
    )

    own = pack[None]
    outer = jnp.concatenate([swap(own, "space", 1), swap_outer(own)], axis=0)
    own_group, order = spread([own], powers(n_leaf), "leaf")
    outer_group, _ = spread([outer], powers(n_leaf), "leaf")
    sizes = tuple(a.shape[0] for a in own_group + outer_group)

    places = tuple((0, m) for m in order) + tuple((kind, m) for m in order for kind in (1, 2))
    table_rows = 3 * n_leaf * (leaf_dev + one_dev) + 1

    far = call(
        functools.partial(couple_kernel, counts, sizes, places, targets, slots),
        [SMEM, VMEM] + [VMEM] * len(sizes),
        jax.ShapeDtypeStruct((targets + 1, width, rank), F32),
        [pltpu.VMEM((table_rows, 24, 128), BF16)] + [pltpu.VMEM((rank, CHUNK * rank), F32)] * (2 * UNROLL),
        2**34,
        (rows.reshape(-1), main, *own_group, *outer_group),
    )

    two = jnp.concatenate([a[:, :, split_at:] for a in own_group], axis=0)
    two_group, two_order = [two], [0]
    for mask in powers(n_space):
        two_group = [jnp.concatenate(two_group + [swap(two_group[0], "space", mask)], axis=0)]
        two_order = two_order + [m ^ mask for m in two_order]
    two_places = tuple((sm, lm) for sm in two_order for lm in order)
    n_two = n_space * n_leaf * two_dev
    return call(
        functools.partial(down_kernel, counts, two_places, slots),
        [SMEM] + [VMEM] * 6,
        jax.ShapeDtypeStruct((width, leaf_dev * leaf_size), BF16),
        [pltpu.VMEM((n_two + 1, 24, 128), BF16)],
        2**24,
        (rows_two.reshape(-1), top, two_group[0], far, basis, t_one, t_two),
    )


def solution(mesh):
    return jax.shard_map(
        local_body,
        mesh=mesh,
        in_specs=(
            P(None, ("space", "leaf")),
            P(("space", "leaf"), None, None),
            P(("space", "leaf"), None, None),
            P(("space", "leaf"), None, None),
            P(("space", "leaf"), None, None),
            P(("space", "leaf"), None, None),
            P(("space", "leaf"), None, None),
            P(("space", "leaf"), None),
            P(("space", "leaf"), None),
            P(("space", "leaf"), None),
        ),
        out_specs=P(None, ("space", "leaf")),
        check_vma=False,
    )
```

```python
import functools

import jax
import jax.numpy as jnp
from jax import lax
from jax.experimental import pallas as pl
from jax.experimental.pallas import tpu as pltpu
from jax.sharding import PartitionSpec as P


LOG2E = 1.4426950408889634
SCALE = 0.75
AMPLITUDE = 0.25
CHUNK = 16
UNROLL = 6
F32 = jnp.float32
BF16 = jnp.bfloat16
NT = (((1,), (1,)), ((), ()))


def dot_nt(a, b):
    return lax.dot_general(a, b, NT, preferred_element_type=F32)


def low_half(shape):
    return lax.broadcasted_iota(jnp.int32, shape, 1) < shape[1] // 2


def wide_nodes(ref, pair, count):
    if ref.shape[0] == count:
        parts = [ref[min(2 * pair + side, count - 1)] for side in range(2)]
    else:
        parts = [ref[:, 2 * pair + side, :] for side in range(2)]
    return jnp.concatenate([part.astype(F32) for part in parts], axis=1)


def split(value):
    high = value.astype(BF16).astype(F32)
    rest = value - high
    middle = rest.astype(BF16).astype(F32)
    return high, middle, rest - middle


def norm_of(nodes):
    square = nodes * nodes
    return (square[0:1] + square[1:2] + square[2:3]) * SCALE


def up_kernel(counts, charges, basis, t_one, t_two, n_leaf, n_one, n_two, pack):
    leaf_dev, one_dev, two_dev = counts
    lanes = 0
    for nodes_ref, count in ((n_leaf, leaf_dev), (n_one, one_dev), (n_two, two_dev)):
        for pair in range((count + 1) // 2):
            nodes = wide_nodes(nodes_ref, pair, count)
            ones = jnp.ones((2, 128), F32)
            rows = jnp.concatenate([nodes, *split(norm_of(nodes)), ones], axis=0)
            pack[0:8, lanes : lanes + 128] = rows.astype(BF16)
            lanes += 128
    half = low_half((16, 128))
    for pair in range(leaf_dev // 2):
        at = pair * 256
        both = jnp.concatenate([charges[:, at : at + 128], charges[:, at + 128 : at + 256]], axis=0)
        coef = dot_nt(both, basis[pair * 128 : pair * 128 + 128, :])
        coef = jnp.where(half, coef[:16], coef[16:])
        pack[8:24, pair * 128 : pair * 128 + 128] = coef.astype(BF16)
    start = leaf_dev * 64
    for pair in range(one_dev // 2):
        at = pair * 1024
        both = jnp.concatenate([pack[8:24, at : at + 512], pack[8:24, at + 512 : at + 1024]], axis=0)
        coef = dot_nt(both, t_one[pair * 128 : pair * 128 + 128, :])
        coef = jnp.where(half, coef[:16], coef[16:])
        pack[8:24, start + pair * 128 : start + pair * 128 + 128] = coef.astype(BF16)
    below, start = start, start + one_dev * 64
    for pair in range((two_dev + 1) // 2):
        parts = []
        for q in range(2 * pair, 2 * pair + 2):
            q = min(q, two_dev - 1)
            children = pack[8:24, below + q * 512 : below + q * 512 + 512]
            parts.append(dot_nt(children, t_two[q * 64 : q * 64 + 64, :]))
        coef = jnp.concatenate(parts, axis=1)
        pack[8:24, start + pair * 128 : start + pair * 128 + 128] = coef.astype(BF16)


def odd_slot(shape):
    return lax.broadcasted_iota(jnp.int32, shape, 1) % 2


def prepare_kernel(counts, n_leaf, n_one, n_two, l_leaf, l_one, l_two, gate, main, top, rows, rows_two):
    del gate
    leaf_dev, one_dev, two_dev = counts
    row = 0
    for nodes_ref, count, out in ((n_leaf, leaf_dev, main), (n_one, one_dev, main), (n_two, two_dev, top)):
        if out is top:
            row = 0
        for pair in range((count + 1) // 2):
            nodes = wide_nodes(nodes_ref, pair, count)
            cross = nodes * (-2.0 * SCALE)
            high = cross.astype(BF16).astype(F32)
            n1, n2, n3 = split(norm_of(nodes))
            one = jnp.ones((3, 128), F32)
            zero = jnp.zeros((3, 128), F32)
            tile = jnp.concatenate([high, one, n1, n2, cross - high, zero, n3, zero[0:1]], axis=0)
            out[row : row + 128, :] = tile.T.astype(BF16)
            row += 128
    slots = l_leaf.shape[1]
    axis_leaf = lax.axis_size("leaf")
    first = (lax.axis_index("space") - 1) * axis_leaf
    leaf_rows, one_rows = 3 * axis_leaf * leaf_dev, 3 * axis_leaf * one_dev
    empty = leaf_rows + one_rows
    total = jnp.zeros((1, 1), jnp.int32)
    start = 0
    for ref, shift in ((l_leaf, -first * leaf_dev), (l_one, leaf_rows - first * one_dev)):
        links = ref[...]
        live = links >= 0
        count = jnp.sum(jnp.where(live, 1.0, 0.0), axis=1, keepdims=True).astype(jnp.int32)
        chunks = jnp.maximum((count + (CHUNK - 1)) // CHUNK, 1)
        total = total + jnp.sum(chunks.astype(F32), axis=0, keepdims=True).astype(jnp.int32)
        end = start + links.shape[0]
        rows[start:end, 0:slots] = jnp.where(live, links + shift, empty) ^ odd_slot(links.shape)
        rows[start:end, slots:] = jnp.broadcast_to(chunks, (links.shape[0], 128 - slots))
        start = end
    rows[start : start + 8, :] = jnp.broadcast_to(total, (8, 128))
    n_top = lax.axis_size("space") * axis_leaf * two_dev
    links = l_two[...]
    flip = odd_slot(links.shape) if two_dev > 1 else 0
    rows_two[:, 0:slots] = jnp.where(links >= 0, links, n_top) ^ flip
    rows_two[:, slots:] = jnp.zeros((two_dev, 128 - slots), jnp.int32)


def matern(square):
    value = jnp.maximum(square, 1e-30)
    r = value * lax.rsqrt(value)
    return (r + 1.0) * jnp.exp2(r * (-LOG2E))


def gather_features(table, links, base, half):
    tiles = []
    for g in range(CHUNK // 2):
        first, second = links[base + 2 * g], links[base + 2 * g + 1]
        tile = jnp.where(half, table[first, 0:8, :], table[second, 0:8, :])
        tiles.append(jnp.concatenate([tile, tile], axis=0))
    return jnp.concatenate(tiles, axis=1)


def gather_coefs(table, links, base, half):
    tiles = []
    for g in range(CHUNK // 2):
        first, second = links[base + 2 * g], links[base + 2 * g + 1]
        tiles.append(jnp.where(half, table[first, 8:24, :], table[second, 8:24, :]))
    return jnp.concatenate(tiles, axis=1)


def put_pair(table, row, tile):
    table[row] = tile
    table[row + 1] = jnp.concatenate([tile[:, 64:], tile[:, :64]], axis=1)


def couple_kernel(counts, sizes, places, targets, slots, links, features, *refs):
    leaf_dev, one_dev, _ = counts
    axis_leaf = lax.axis_size("leaf")
    my_leaf = lax.axis_index("leaf")
    parity = lax.axis_index("space") % 2
    side_of = (jnp.int32(1), 2 - 2 * parity, 2 * parity)
    starts = (0, 3 * axis_leaf * leaf_dev)
    blocks, far = refs[: len(sizes)], refs[len(sizes)]
    table = refs[len(sizes) + 1]
    dbufs = refs[len(sizes) + 2 : len(sizes) + 2 + UNROLL]
    kbufs = refs[len(sizes) + 2 + UNROLL :]
    far[...] = jnp.zeros_like(far)
    for row in range(table.shape[0] - 2, table.shape[0]):
        table[row] = jnp.zeros((24, 128), BF16)
    at = 0
    spread_by = 32 if len(places) <= 12 else 4
    for ref, size in zip(blocks, sizes):
        for index in range(size):
            kind, mask = places[at]
            device = side_of[kind] * axis_leaf + (my_leaf ^ mask)
            for first, count, start in ((0, leaf_dev, starts[0]), (leaf_dev, one_dev, starts[1])):
                base = start + device * count

                def one_pair(pair, carry, ref=ref, index=index, first=first, base=base):
                    lane = pl.multiple_of((first // 2 + pair) * 128, 128)
                    put_pair(table, base + 2 * pair, ref[index, :, pl.ds(lane, 128)])
                    return carry

                lax.fori_loop(0, count // 2, one_pair, 0, unroll=min(spread_by, count // 2))
            at += 1
    half8 = low_half((8, 128))
    half16 = low_half((16, 128))
    last_target = targets - 1

    def step(u, state):
        t0, c0, t1, b1, t2, b2 = state
        d_in, d_out = dbufs[u - 1], dbufs[u]
        k_in, k_out = kbufs[u - 1], kbufs[u]
        tt = jnp.minimum(t0, last_target)
        b0 = tt * 128 + c0 * CHUNK
        row = pl.multiple_of(tt * 64, 64)
        d_out[...] = jnp.dot(
            features[pl.ds(row, 64), :],
            gather_features(table, links, b0, half8),
            preferred_element_type=F32,
        )
        coefs = gather_coefs(table, links, b2, half16)
        far[t2] = far[t2] + dot_nt(coefs, k_in[...].astype(BF16))
        for g in range(CHUNK // 2):
            k_out[:, g * 128 : g * 128 + 128] = matern(d_in[:, g * 128 : g * 128 + 128])
        last = c0 + 1 >= links[tt * 128 + slots]
        next_t = jnp.where(last, jnp.minimum(t0 + 1, targets), t0)
        next_c = jnp.where(last, 0, c0 + 1)
        return next_t, next_c, t0, b0, t1, b1

    def body(_, state):
        for u in range(UNROLL):
            state = step(u, state)
        return state

    zero, none = jnp.int32(0), jnp.int32(targets)
    total = links[targets * 128]
    lax.fori_loop(0, (total + 2 + UNROLL - 1) // UNROLL, body, (zero, zero, none, zero, none, zero))


def down_kernel(counts, places, slots, links, features, blocks, far, basis, t_one, t_two, out, table):
    leaf_dev, _, two_dev = counts
    pairs = (two_dev + 1) // 2
    for row in range(table.shape[0] - 2, table.shape[0]):
        table[row] = jnp.zeros((24, 128), BF16)
    axis_leaf = lax.axis_size("leaf")
    my_space, my_leaf = lax.axis_index("space"), lax.axis_index("leaf")
    for index, (space_mask, leaf_mask) in enumerate(places):
        base = ((my_space ^ space_mask) * axis_leaf + (my_leaf ^ leaf_mask)) * two_dev
        for pair in range(pairs):
            tile = blocks[index, :, pair * 128 : pair * 128 + 128]
            if two_dev > 1:
                put_pair(table, base + 2 * pair, tile)
            else:
                table[base] = tile
    half8 = low_half((8, 128))
    half16 = low_half((16, 128))
    for q in range(two_dev):
        far_two = jnp.zeros((16, 64), F32)
        for c in range(slots // CHUNK):
            base = q * 128 + c * CHUNK
            square = jnp.dot(
                features[q * 64 : q * 64 + 64, :],
                gather_features(table, links, base, half8),
                preferred_element_type=F32,
            )
            far_two += dot_nt(gather_coefs(table, links, base, half16), matern(square).astype(BF16))
        local_two = (far_two * AMPLITUDE).astype(BF16)
        down_one = jnp.dot(local_two, t_two[q * 64 : q * 64 + 64, :], preferred_element_type=F32)
        for i in range(8):
            p = q * 8 + i
            local_one = far[leaf_dev + p] * AMPLITUDE + down_one[:, i * 64 : i * 64 + 64]
            down_leaf = jnp.dot(
                local_one.astype(BF16), t_one[p * 64 : p * 64 + 64, :], preferred_element_type=F32
            )
            for j in range(8):
                t = p * 8 + j
                local_leaf = far[t] * AMPLITUDE + down_leaf[:, j * 64 : j * 64 + 64]
                out[:, t * 128 : t * 128 + 128] = jnp.dot(
                    local_leaf.astype(BF16), basis[t * 64 : t * 64 + 64, :], preferred_element_type=F32
                ).astype(BF16)


VMEM = pl.BlockSpec(memory_space=pltpu.VMEM)
SMEM = pl.BlockSpec(memory_space=pltpu.SMEM)


def padded(shape, dtype):
    rows = -(-shape[-2] // 8) * 8 if len(shape) > 1 else 1
    size = rows * (-(-shape[-1] // 128) * 128) * jnp.dtype(dtype).itemsize
    for extent in shape[:-2]:
        size *= extent
    return size


def call(kernel, name, specs, out, scratch, flops, args):
    moved = sum(a.size * a.dtype.itemsize for a in args)
    held = [a for a, spec in zip(args, specs) if spec is VMEM] + jax.tree.leaves(out)
    held_only = name != "up"
    limit = sum(padded(a.shape, a.dtype) for a in held) + sum(padded(a.shape, a.dtype) for a in scratch)
    return pl.pallas_call(
        kernel,
        out_shape=out,
        in_specs=specs,
        out_specs=jax.tree.map(lambda _: VMEM, out),
        scratch_shapes=scratch,
        cost_estimate=pl.CostEstimate(flops=flops, bytes_accessed=moved, transcendentals=0),
        compiler_params=pltpu.CompilerParams(vmem_limit_bytes=min(limit + 6 * 2**20, 60 * 2**20) if held_only else 60 * 2**20),
    )(*args)


def swap(value, axis, mask):
    count = lax.axis_size(axis)
    return lax.ppermute(value, axis, [(i, i ^ mask) for i in range(count)])


def relay(near):
    count = lax.axis_size("space")
    pairs = []
    for s in range(count):
        if s % 2:
            pairs.append((s, s - 2 if s >= 3 else 0))
        else:
            pairs.append((s, s + 2 if s + 2 < count else count - 1))
    return lax.ppermute(near, "space", pairs)


def spread(group, masks, axis):
    order = [0]
    for mask in masks:
        merged = group[0] if len(group) == 1 else jnp.concatenate(group, axis=0)
        group = group + [swap(merged, axis, mask)]
        order = order + [m ^ mask for m in order]
    return group, order


def powers(count):
    return [1 << b for b in reversed(range(count.bit_length() - 1))]


def local_body(
    charges,
    leaf_basis,
    transfer_one,
    transfer_two,
    nodes_leaf,
    nodes_one,
    nodes_two,
    links_leaf,
    links_one,
    links_two,
):
    width = charges.shape[0]
    leaf_dev, rank, leaf_size = leaf_basis.shape
    one_dev = leaf_dev // 8
    two_dev = one_dev // 8
    counts = (leaf_dev, one_dev, two_dev)
    slots = links_leaf.shape[1]
    n_space, n_leaf = lax.axis_size("space"), lax.axis_size("leaf")
    two_lanes = (two_dev + 1) // 2 * 128
    split_at = (leaf_dev + one_dev) * rank
    lanes = split_at + two_lanes

    basis = leaf_basis.reshape(leaf_dev * rank, leaf_size)
    t_one = transfer_one.reshape(one_dev * rank, 8 * rank)
    t_two = transfer_two.reshape(two_dev * rank, 8 * rank)
    nodes_leaf, nodes_one = jnp.swapaxes(nodes_leaf, 0, 1), jnp.swapaxes(nodes_one, 0, 1)
    pack = call(
        functools.partial(up_kernel, counts),
        "up",
        [VMEM] * 7,
        jax.ShapeDtypeStruct((24, lanes), BF16),
        [],
        2 * leaf_dev * rank * leaf_size * width,
        (charges, basis, t_one, t_two, nodes_leaf, nodes_one, nodes_two),
    )
    targets = leaf_dev + one_dev
    main, top, rows, rows_two = call(
        functools.partial(prepare_kernel, counts),
        "prepare",
        [VMEM] * 6 + [pl.BlockSpec(memory_space=pl.ANY)],
        (
            jax.ShapeDtypeStruct((targets * rank, 16), BF16),
            jax.ShapeDtypeStruct((two_lanes, 16), BF16),
            jax.ShapeDtypeStruct((targets + 8, 128), jnp.int32),
            jax.ShapeDtypeStruct((two_dev, 128), jnp.int32),
        ),
        [],
        2**32,
        (nodes_leaf, nodes_one, nodes_two, links_leaf, links_one, links_two, pack),
    )

    own = pack[None]
    near = swap(own, "space", 1)
    far_side = relay(near)
    own_group, order = spread([own], powers(n_leaf), "leaf")
    near_group, _ = spread([near], powers(n_leaf), "leaf")
    far_group, _ = spread([far_side], powers(n_leaf), "leaf")
    received = own_group + near_group + far_group
    sizes = tuple(a.shape[0] for a in received)
    places = tuple((kind, m) for kind in range(3) for m in order)
    table_rows = 3 * n_leaf * (leaf_dev + one_dev) + 2

    far = call(
        functools.partial(couple_kernel, counts, sizes, places, targets, slots),
        "couple",
        [SMEM, VMEM] + [VMEM] * len(sizes),
        jax.ShapeDtypeStruct((targets + 1, width, rank), F32),
        [pltpu.VMEM((table_rows, 24, 128), BF16)] + [pltpu.VMEM((rank, CHUNK * rank), F32)] * (2 * UNROLL),
        2**34,
        (rows.reshape(-1), main, *received),
    )

    two = jnp.concatenate([a[:, :, split_at:] for a in own_group], axis=0)
    two_group, two_order = [two], [0]
    for mask in powers(n_space):
        two_group = [jnp.concatenate(two_group + [swap(two_group[0], "space", mask)], axis=0)]
        two_order = two_order + [m ^ mask for m in two_order]
    two_places = tuple((sm, lm) for sm in two_order for lm in order)
    n_two = n_space * n_leaf * two_dev
    return call(
        functools.partial(down_kernel, counts, two_places, slots),
        "down",
        [SMEM] + [VMEM] * 6,
        jax.ShapeDtypeStruct((width, leaf_dev * leaf_size), BF16),
        [pltpu.VMEM((n_two + 2, 24, 128), BF16)],
        2**24,
        (rows_two.reshape(-1), top, two_group[0], far, basis, t_one, t_two),
    )


def solution(mesh):
    return jax.shard_map(
        local_body,
        mesh=mesh,
        in_specs=(
            P(None, ("space", "leaf")),
            P(("space", "leaf"), None, None),
            P(("space", "leaf"), None, None),
            P(("space", "leaf"), None, None),
            P(("space", "leaf"), None, None),
            P(("space", "leaf"), None, None),
            P(("space", "leaf"), None, None),
            P(("space", "leaf"), None),
            P(("space", "leaf"), None),
            P(("space", "leaf"), None),
        ),
        out_specs=P(None, ("space", "leaf")),
        check_vma=False,
    )
```

```python
import functools

import jax
import jax.numpy as jnp
from jax import lax
from jax.experimental import pallas as pl
from jax.experimental.pallas import tpu as pltpu
from jax.sharding import PartitionSpec as P


LOG2E = 1.4426950408889634
SCALE = 0.75
AMPLITUDE = 0.25
CHUNK = 16
UNROLL = 8
F32 = jnp.float32
BF16 = jnp.bfloat16
NT = (((1,), (1,)), ((), ()))


def dot_nt(a, b):
    return lax.dot_general(a, b, NT, preferred_element_type=F32)


def low_half(shape):
    return lax.broadcasted_iota(jnp.int32, shape, 1) < shape[1] // 2


def wide_nodes(ref, pair, count):
    if ref.shape[0] == count:
        parts = [ref[min(2 * pair + side, count - 1)] for side in range(2)]
    else:
        parts = [ref[:, 2 * pair + side, :] for side in range(2)]
    return jnp.concatenate([part.astype(F32) for part in parts], axis=1)


def split(value):
    high = value.astype(BF16).astype(F32)
    rest = value - high
    middle = rest.astype(BF16).astype(F32)
    return high, middle, rest - middle


def norm_of(nodes):
    square = nodes * nodes
    return (square[0:1] + square[1:2] + square[2:3]) * SCALE


def up_kernel(counts, charges, basis, t_one, t_two, n_leaf, n_one, n_two, pack):
    leaf_dev, one_dev, two_dev = counts
    lanes = 0
    for nodes_ref, count in ((n_leaf, leaf_dev), (n_one, one_dev), (n_two, two_dev)):
        for pair in range((count + 1) // 2):
            nodes = wide_nodes(nodes_ref, pair, count)
            ones = jnp.ones((2, 128), F32)
            rows = jnp.concatenate([nodes, *split(norm_of(nodes)), ones], axis=0)
            pack[0:8, lanes : lanes + 128] = rows.astype(BF16)
            lanes += 128
    half = low_half((16, 128))
    for pair in range(leaf_dev // 2):
        at = pair * 256
        both = jnp.concatenate([charges[:, at : at + 128], charges[:, at + 128 : at + 256]], axis=0)
        coef = dot_nt(both, basis[pair * 128 : pair * 128 + 128, :])
        coef = jnp.where(half, coef[:16], coef[16:])
        pack[8:24, pair * 128 : pair * 128 + 128] = coef.astype(BF16)
    start = leaf_dev * 64
    for pair in range(one_dev // 2):
        at = pair * 1024
        both = jnp.concatenate([pack[8:24, at : at + 512], pack[8:24, at + 512 : at + 1024]], axis=0)
        coef = dot_nt(both, t_one[pair * 128 : pair * 128 + 128, :])
        coef = jnp.where(half, coef[:16], coef[16:])
        pack[8:24, start + pair * 128 : start + pair * 128 + 128] = coef.astype(BF16)
    below, start = start, start + one_dev * 64
    for pair in range((two_dev + 1) // 2):
        parts = []
        for q in range(2 * pair, 2 * pair + 2):
            q = min(q, two_dev - 1)
            children = pack[8:24, below + q * 512 : below + q * 512 + 512]
            parts.append(dot_nt(children, t_two[q * 64 : q * 64 + 64, :]))
        coef = jnp.concatenate(parts, axis=1)
        pack[8:24, start + pair * 128 : start + pair * 128 + 128] = coef.astype(BF16)


def odd_slot(shape):
    return lax.broadcasted_iota(jnp.int32, shape, 1) % 2


def prepare_kernel(counts, n_leaf, n_one, n_two, l_leaf, l_one, l_two, gate, main, top, rows, rows_two):
    del gate
    leaf_dev, one_dev, two_dev = counts
    row = 0
    for nodes_ref, count, out in ((n_leaf, leaf_dev, main), (n_one, one_dev, main), (n_two, two_dev, top)):
        if out is top:
            row = 0
        for pair in range((count + 1) // 2):
            nodes = wide_nodes(nodes_ref, pair, count)
            cross = nodes * (-2.0 * SCALE)
            high = cross.astype(BF16).astype(F32)
            n1, n2, n3 = split(norm_of(nodes))
            one = jnp.ones((3, 128), F32)
            zero = jnp.zeros((3, 128), F32)
            tile = jnp.concatenate([high, one, n1, n2, cross - high, zero, n3, zero[0:1]], axis=0)
            out[row : row + 128, :] = tile.T.astype(BF16)
            row += 128
    slots = l_leaf.shape[1]
    axis_leaf = lax.axis_size("leaf")
    first = (lax.axis_index("space") - 1) * axis_leaf
    leaf_rows, one_rows = 3 * axis_leaf * leaf_dev, 3 * axis_leaf * one_dev
    empty = leaf_rows + one_rows
    total = jnp.zeros((1, 1), jnp.int32)
    start = 0
    for ref, shift in ((l_leaf, -first * leaf_dev), (l_one, leaf_rows - first * one_dev)):
        links = ref[...]
        live = links >= 0
        count = jnp.sum(jnp.where(live, 1.0, 0.0), axis=1, keepdims=True).astype(jnp.int32)
        chunks = jnp.maximum((count + (CHUNK - 1)) // CHUNK, 1)
        total = total + jnp.sum(chunks.astype(F32), axis=0, keepdims=True).astype(jnp.int32)
        end = start + links.shape[0]
        rows[start:end, 0:slots] = jnp.where(live, links + shift, empty) ^ odd_slot(links.shape)
        rows[start:end, slots:] = jnp.broadcast_to(chunks, (links.shape[0], 128 - slots))
        start = end
    rows[start : start + 8, :] = jnp.broadcast_to(total, (8, 128))
    n_top = lax.axis_size("space") * axis_leaf * two_dev
    links = l_two[...]
    flip = odd_slot(links.shape) if two_dev > 1 else 0
    rows_two[:, 0:slots] = jnp.where(links >= 0, links, n_top) ^ flip
    rows_two[:, slots:] = jnp.zeros((two_dev, 128 - slots), jnp.int32)


def matern(square):
    value = jnp.maximum(square, 1e-30)
    r = value * lax.rsqrt(value)
    return (r + 1.0) * jnp.exp2(r * (-LOG2E))


def gather_features(table, links, base, half):
    tiles = []
    for g in range(CHUNK // 2):
        first, second = links[base + 2 * g], links[base + 2 * g + 1]
        tile = jnp.where(half, table[first, 0:8, :], table[second, 0:8, :])
        tiles.append(jnp.concatenate([tile, tile], axis=0))
    return jnp.concatenate(tiles, axis=1)


def gather_coefs(table, links, base, half):
    tiles = []
    for g in range(CHUNK // 2):
        first, second = links[base + 2 * g], links[base + 2 * g + 1]
        tiles.append(jnp.where(half, table[first, 8:24, :], table[second, 8:24, :]))
    return jnp.concatenate(tiles, axis=1)


def put_pair(table, row, tile):
    table[row] = tile
    table[row + 1] = jnp.concatenate([tile[:, 64:], tile[:, :64]], axis=1)


def couple_kernel(counts, sizes, places, targets, slots, links, features, *refs):
    leaf_dev, one_dev, _ = counts
    axis_leaf = lax.axis_size("leaf")
    my_leaf = lax.axis_index("leaf")
    parity = lax.axis_index("space") % 2
    side_of = (jnp.int32(1), 2 - 2 * parity, 2 * parity)
    starts = (0, 3 * axis_leaf * leaf_dev)
    blocks, far = refs[: len(sizes)], refs[len(sizes)]
    table = refs[len(sizes) + 1]
    dbufs = refs[len(sizes) + 2 : len(sizes) + 2 + UNROLL]
    kbufs = refs[len(sizes) + 2 + UNROLL :]
    far[...] = jnp.zeros_like(far)
    for row in range(table.shape[0] - 2, table.shape[0]):
        table[row] = jnp.zeros((24, 128), BF16)
    at = 0
    spread_by = 32 if len(places) <= 12 else 4
    for ref, size in zip(blocks, sizes):
        for index in range(size):
            kind, mask = places[at]
            device = side_of[kind] * axis_leaf + (my_leaf ^ mask)
            for first, count, start in ((0, leaf_dev, starts[0]), (leaf_dev, one_dev, starts[1])):
                base = start + device * count

                def one_pair(pair, carry, ref=ref, index=index, first=first, base=base):
                    lane = pl.multiple_of((first // 2 + pair) * 128, 128)
                    put_pair(table, base + 2 * pair, ref[index, :, pl.ds(lane, 128)])
                    return carry

                lax.fori_loop(0, count // 2, one_pair, 0, unroll=min(spread_by, count // 2))
            at += 1
    half8 = low_half((8, 128))
    half16 = low_half((16, 128))
    last_target = targets - 1

    def step(u, state):
        t0, c0, t1, b1, t2, b2 = state
        d_in, d_out = dbufs[u - 1], dbufs[u]
        k_in, k_out = kbufs[u - 1], kbufs[u]
        tt = jnp.minimum(t0, last_target)
        b0 = tt * 128 + c0 * CHUNK
        row = pl.multiple_of(tt * 64, 64)
        d_out[...] = jnp.dot(
            features[pl.ds(row, 64), :],
            gather_features(table, links, b0, half8),
            preferred_element_type=F32,
        )
        coefs = gather_coefs(table, links, b2, half16)
        far[t2] = far[t2] + dot_nt(coefs, k_in[...].astype(BF16))
        for g in range(CHUNK // 2):
            k_out[:, g * 128 : g * 128 + 128] = matern(d_in[:, g * 128 : g * 128 + 128])
        last = c0 + 1 >= links[tt * 128 + slots]
        next_t = jnp.where(last, jnp.minimum(t0 + 1, targets), t0)
        next_c = jnp.where(last, 0, c0 + 1)
        return next_t, next_c, t0, b0, t1, b1

    def body(_, state):
        for u in range(UNROLL):
            state = step(u, state)
        return state

    zero, none = jnp.int32(0), jnp.int32(targets)
    total = links[targets * 128]
    lax.fori_loop(0, (total + 2 + UNROLL - 1) // UNROLL, body, (zero, zero, none, zero, none, zero))


def down_kernel(counts, places, slots, links, features, blocks, far, basis, t_one, t_two, out, table):
    leaf_dev, _, two_dev = counts
    pairs = (two_dev + 1) // 2
    for row in range(table.shape[0] - 2, table.shape[0]):
        table[row] = jnp.zeros((24, 128), BF16)
    axis_leaf = lax.axis_size("leaf")
    my_space, my_leaf = lax.axis_index("space"), lax.axis_index("leaf")
    for index, (space_mask, leaf_mask) in enumerate(places):
        base = ((my_space ^ space_mask) * axis_leaf + (my_leaf ^ leaf_mask)) * two_dev
        for pair in range(pairs):
            tile = blocks[index, :, pair * 128 : pair * 128 + 128]
            if two_dev > 1:
                put_pair(table, base + 2 * pair, tile)
            else:
                table[base] = tile
    half8 = low_half((8, 128))
    half16 = low_half((16, 128))
    for q in range(two_dev):
        far_two = jnp.zeros((16, 64), F32)
        for c in range(slots // CHUNK):
            base = q * 128 + c * CHUNK
            square = jnp.dot(
                features[q * 64 : q * 64 + 64, :],
                gather_features(table, links, base, half8),
                preferred_element_type=F32,
            )
            far_two += dot_nt(gather_coefs(table, links, base, half16), matern(square).astype(BF16))
        local_two = (far_two * AMPLITUDE).astype(BF16)
        down_one = jnp.dot(local_two, t_two[q * 64 : q * 64 + 64, :], preferred_element_type=F32)
        for i in range(8):
            p = q * 8 + i
            local_one = far[leaf_dev + p] * AMPLITUDE + down_one[:, i * 64 : i * 64 + 64]
            down_leaf = jnp.dot(
                local_one.astype(BF16), t_one[p * 64 : p * 64 + 64, :], preferred_element_type=F32
            )
            for j in range(8):
                t = p * 8 + j
                local_leaf = far[t] * AMPLITUDE + down_leaf[:, j * 64 : j * 64 + 64]
                out[:, t * 128 : t * 128 + 128] = jnp.dot(
                    local_leaf.astype(BF16), basis[t * 64 : t * 64 + 64, :], preferred_element_type=F32
                ).astype(BF16)


VMEM = pl.BlockSpec(memory_space=pltpu.VMEM)
SMEM = pl.BlockSpec(memory_space=pltpu.SMEM)


def padded(shape, dtype):
    rows = -(-shape[-2] // 8) * 8 if len(shape) > 1 else 1
    size = rows * (-(-shape[-1] // 128) * 128) * jnp.dtype(dtype).itemsize
    for extent in shape[:-2]:
        size *= extent
    return size


def call(kernel, name, specs, out, scratch, flops, args):
    moved = sum(a.size * a.dtype.itemsize for a in args)
    held = [a for a, spec in zip(args, specs) if spec is VMEM] + jax.tree.leaves(out)
    held_only = name != "up"
    limit = sum(padded(a.shape, a.dtype) for a in held) + sum(padded(a.shape, a.dtype) for a in scratch)
    return pl.pallas_call(
        kernel,
        out_shape=out,
        in_specs=specs,
        out_specs=jax.tree.map(lambda _: VMEM, out),
        scratch_shapes=scratch,
        cost_estimate=pl.CostEstimate(flops=flops, bytes_accessed=moved, transcendentals=0),
        compiler_params=pltpu.CompilerParams(vmem_limit_bytes=min(limit + 6 * 2**20, 60 * 2**20) if held_only else 60 * 2**20),
    )(*args)


def swap(value, axis, mask):
    count = lax.axis_size(axis)
    return lax.ppermute(value, axis, [(i, i ^ mask) for i in range(count)])


def relay(near):
    count = lax.axis_size("space")
    pairs = []
    for s in range(count):
        if s % 2:
            pairs.append((s, s - 2 if s >= 3 else 0))
        else:
            pairs.append((s, s + 2 if s + 2 < count else count - 1))
    return lax.ppermute(near, "space", pairs)


def spread(group, masks, axis):
    order = [0]
    for mask in masks:
        merged = group[0] if len(group) == 1 else jnp.concatenate(group, axis=0)
        group = group + [swap(merged, axis, mask)]
        order = order + [m ^ mask for m in order]
    return group, order


def powers(count):
    return [1 << b for b in reversed(range(count.bit_length() - 1))]


def local_body(
    charges,
    leaf_basis,
    transfer_one,
    transfer_two,
    nodes_leaf,
    nodes_one,
    nodes_two,
    links_leaf,
    links_one,
    links_two,
):
    width = charges.shape[0]
    leaf_dev, rank, leaf_size = leaf_basis.shape
    one_dev = leaf_dev // 8
    two_dev = one_dev // 8
    counts = (leaf_dev, one_dev, two_dev)
    slots = links_leaf.shape[1]
    n_space, n_leaf = lax.axis_size("space"), lax.axis_size("leaf")
    two_lanes = (two_dev + 1) // 2 * 128
    split_at = (leaf_dev + one_dev) * rank
    lanes = split_at + two_lanes

    basis = leaf_basis.reshape(leaf_dev * rank, leaf_size)
    t_one = transfer_one.reshape(one_dev * rank, 8 * rank)
    t_two = transfer_two.reshape(two_dev * rank, 8 * rank)
    nodes_leaf, nodes_one = jnp.swapaxes(nodes_leaf, 0, 1), jnp.swapaxes(nodes_one, 0, 1)
    pack = call(
        functools.partial(up_kernel, counts),
        "up",
        [VMEM] * 7,
        jax.ShapeDtypeStruct((24, lanes), BF16),
        [],
        2 * leaf_dev * rank * leaf_size * width,
        (charges, basis, t_one, t_two, nodes_leaf, nodes_one, nodes_two),
    )
    targets = leaf_dev + one_dev
    main, top, rows, rows_two = call(
        functools.partial(prepare_kernel, counts),
        "prepare",
        [VMEM] * 6 + [pl.BlockSpec(memory_space=pl.ANY)],
        (
            jax.ShapeDtypeStruct((targets * rank, 16), BF16),
            jax.ShapeDtypeStruct((two_lanes, 16), BF16),
            jax.ShapeDtypeStruct((targets + 8, 128), jnp.int32),
            jax.ShapeDtypeStruct((two_dev, 128), jnp.int32),
        ),
        [],
        2**32,
        (nodes_leaf, nodes_one, nodes_two, links_leaf, links_one, links_two, pack),
    )

    own = pack[None]
    near = swap(own, "space", 1)
    far_side = relay(near)
    own_group, order = spread([own], powers(n_leaf), "leaf")
    masks = powers(n_leaf)
    last = masks[-1]
    near_group, part = spread([near], masks[:-1], "leaf")
    far_group, _ = spread([far_side], masks[:-1], "leaf")
    crossed = swap(jnp.concatenate(near_group + [far_side], axis=0), "leaf", last)
    remaining = far_group[1] if len(far_group) == 2 else jnp.concatenate(far_group[1:], axis=0)
    rest = swap(remaining, "leaf", last)
    received = own_group + near_group + [crossed] + far_group + [rest]
    sizes = tuple(a.shape[0] for a in received)
    places = tuple((0, m) for m in order) + tuple((1, m) for m in part) + tuple((1, m ^ last) for m in part)
    places += ((2, last),) + tuple((2, m) for m in part) + tuple((2, m ^ last) for m in part[1:])

    table_rows = 3 * n_leaf * (leaf_dev + one_dev) + 2

    far = call(
        functools.partial(couple_kernel, counts, sizes, places, targets, slots),
        "couple",
        [SMEM, VMEM] + [VMEM] * len(sizes),
        jax.ShapeDtypeStruct((targets + 1, width, rank), F32),
        [pltpu.VMEM((table_rows, 24, 128), BF16)] + [pltpu.VMEM((rank, CHUNK * rank), F32)] * (2 * UNROLL),
        2**34,
        (rows.reshape(-1), main, *received),
    )

    two = jnp.concatenate([a[:, :, split_at:] for a in own_group], axis=0)
    two_group, two_order = [two], [0]
    for mask in powers(n_space):
        two_group = [jnp.concatenate(two_group + [swap(two_group[0], "space", mask)], axis=0)]
        two_order = two_order + [m ^ mask for m in two_order]
    two_places = tuple((sm, lm) for sm in two_order for lm in order)
    n_two = n_space * n_leaf * two_dev
    return call(
        functools.partial(down_kernel, counts, two_places, slots),
        "down",
        [SMEM] + [VMEM] * 6,
        jax.ShapeDtypeStruct((width, leaf_dev * leaf_size), BF16),
        [pltpu.VMEM((n_two + 2, 24, 128), BF16)],
        2**24,
        (rows_two.reshape(-1), top, two_group[0], far, basis, t_one, t_two),
    )


def solution(mesh):
    return jax.shard_map(
        local_body,
        mesh=mesh,
        in_specs=(
            P(None, ("space", "leaf")),
            P(("space", "leaf"), None, None),
            P(("space", "leaf"), None, None),
            P(("space", "leaf"), None, None),
            P(("space", "leaf"), None, None),
            P(("space", "leaf"), None, None),
            P(("space", "leaf"), None, None),
            P(("space", "leaf"), None),
            P(("space", "leaf"), None),
            P(("space", "leaf"), None),
        ),
        out_specs=P(None, ("space", "leaf")),
        check_vma=False,
    )
```
